32 devices in a mesh: parts: 2 (over x), view: 8 (over z, y), slab: 2 (over core).
Axes of the slice: x: 2, y: 2, z: 4, core: 2. Of those that a mesh axis runs over, the one named last changes fastest.
Arguments:
- activity: bfloat16 [128, 32, 256], P(('parts', 'view'), 'slab'), parts along dimension 0, may hold values from 0.6 to 11.2
- histo_counts: int32 [32, 64, 32, 256], P(('parts', 'view'), None, 'slab'), parts along dimension 0, may hold values from 0 to 22
- background: bfloat16 [32, 32, 256], P(('parts', 'view'), 'slab'), parts along dimension 0, may hold values from 0.5 to 2
- blur_values: bfloat16 [16, 3, 256, 32], P('view'), may hold values from 0.0041503906 to 0.020751953
- band_start: int32 [16, 3, 256], P('view'), may hold values from 0 to 224, as said below
Outputs:
- gradient: float32 [128, 32, 256], P(('parts', 'view'), 'slab'), parts along dimension 0
The draws below stay inside these ranges and needn't reach their ends.
There are 2 independent parts, one for each index of `parts`. The reference program is written for one: setup_inputs(seed, part) draws one part's arguments, and reference() takes and returns one part's arrays. A program takes and returns all parts, laid end to end along the dimension named above; an argument that names none is the same for every part. Nothing has to cross between parts.
Inputs may be any that keep to these rules, and one draw needn't show every extreme that they name: Each band lies inside the matrix: columns band_start to band_start + 31.
All inputs are finite; a program needn't handle non-finite values.
Results may differ from the reference program's by a relative error of at most 0.0003.
Values may be sent and summed in bfloat16 or wider, within the bound.
A program may use at most 64 MiB of HBM per device.

```python
import math
import jax
import jax.numpy as jnp
from jax import lax

NX = 256
BAND = 32
TAPS = 3
NY = 64
NZ = 32
VIEWS = 16


def level_grid(key):
    keyed = jax.random.fold_in(key, 11)
    levels = jax.random.randint(keyed, (NY, NZ), 0, 7)
    return levels.at[0, 0].set(6).astype(jnp.int32)


def draw_activity(key, part):
    levels = level_grid(key)
    scales = jnp.exp2(levels.astype(jnp.float32) * 0.5)
    uniform_part = jax.random.uniform(jax.random.fold_in(key, 13), (NY, NZ, NX), jnp.float32)
    factor = 0.6 + 0.8 * uniform_part
    return (scales[:, :, None] * factor).astype(jnp.bfloat16)


def draw_histo_counts(key, part):
    levels = level_grid(key)
    table = jnp.array([2, 3, 4, 5, 6, 8, 11], jnp.int32)
    means = table[levels]
    upper = 2 * means[None, :, :, None] + 1
    counts = jax.random.randint(jax.random.fold_in(key, 17), (VIEWS, NY, NZ, NX), 0, upper)
    counts = counts.at[0, 0, 0, 0].set(22)
    counts = counts.at[0, 0, 0, 1].set(0)
    return counts.astype(jnp.int32)


def draw_band_start(key, part):
    keyed = jax.random.fold_in(key, 7)
    first_key, second_key = jax.random.split(keyed)
    reach = max(BAND // 4, 1)
    offsets = jax.random.randint(first_key, (VIEWS, TAPS, 1), -reach, reach + 1)
    jitters = jax.random.randint(second_key, (VIEWS, TAPS, NX), -1, 2)
    positions = jnp.arange(NX, dtype=jnp.int32)[None, None, :]
    return jnp.clip(positions - BAND // 2 + offsets + jitters, 0, NX - BAND).astype(jnp.int32)


def level_of(rng, dims, shards, smallest, largest):
    level = 1.0
    for axis_at, shards_of in shards:
        heights = jax.random.uniform(jax.random.fold_in(jax.random.fold_in(rng, 6), axis_at), (shards_of,), jnp.float32, smallest / len(shards), largest / len(shards))
        level = level * jnp.repeat(jnp.exp(heights), dims[axis_at] // shards_of).reshape((-1,) + (1,) * (len(dims) - 1 - axis_at))
    return level


def setup_inputs(seed: int = 0, part: int = 0) -> dict:
    seeds = jax.random.split(jax.random.key(seed), 6)
    part_keys = jax.random.split(jax.random.fold_in(seeds[5], part), 6)
    return {
        "activity": draw_activity(jax.random.fold_in(jax.random.fold_in(seeds[5], part), 71), part),
        "histo_counts": draw_histo_counts(jax.random.fold_in(jax.random.fold_in(seeds[5], part), 71), part),
        "background": jnp.clip(jnp.exp(math.log(2.0) - 1.3862944 * jax.random.uniform(part_keys[2], (VIEWS, NZ, NX), jnp.float32) ** level_of(part_keys[2], (VIEWS, NZ, NX), ((0, 8), (1, 2)), -0.2, 0.2)), 0.5, 2.0).astype(jnp.bfloat16),
        "blur_values": jnp.clip(0.0041503906 + 0.016601562 * jax.random.uniform(seeds[3], (VIEWS, TAPS, NX, BAND), jnp.float32) ** level_of(seeds[3], (VIEWS, TAPS, NX, BAND), ((0, 8),), -0.2, 0.2), 0.0041503906, 0.020751953).astype(jnp.bfloat16),
        "band_start": draw_band_start(jax.random.fold_in(seeds[5], 71), part),
    }


def blur_matrix(band_values, band_starts):
    width_x = band_values.shape[0]
    band_width = band_values.shape[1]
    columns = jnp.arange(width_x, dtype=jnp.int32)
    distance = columns[None, :] - band_starts.astype(jnp.int32)[:, None]
    selector = (distance[:, :, None] == jnp.arange(band_width, dtype=jnp.int32)[None, None, :]).astype(jnp.float32)
    return jnp.einsum('ik,ijk->ij', band_values.astype(jnp.float32), selector).astype(jnp.bfloat16)


def view_gradient(activity, view_counts, view_background, view_values, view_starts):
    rows_y, slices, width_x = activity.shape
    matrices = [blur_matrix(view_values[tap_index], view_starts[tap_index]) for tap_index in range(3)]
    padded = jnp.pad(activity, ((0, 0), (1, 1), (0, 0)))
    summed = jnp.zeros((rows_y * slices, width_x), jnp.float32)
    for tap_index in range(3):
        shifted = padded[:, tap_index:tap_index + slices, :].reshape(-1, width_x)
        summed = summed + jnp.dot(shifted, matrices[tap_index].T, preferred_element_type=jnp.float32)
    expected = summed.reshape(rows_y, slices, width_x) + view_background.astype(jnp.float32)[None]
    ratio_bf = (view_counts.astype(jnp.float32) / expected - 1.0).astype(jnp.bfloat16)
    widened = jnp.pad(ratio_bf, ((0, 0), (1, 1), (0, 0)))
    back_sum = jnp.zeros((rows_y * slices, width_x), jnp.float32)
    for tap_index in range(3):
        shifted = widened[:, 2 - tap_index:2 - tap_index + slices, :].reshape(-1, width_x)
        back_sum = back_sum + jnp.dot(shifted, matrices[tap_index], preferred_element_type=jnp.float32)
    return back_sum.reshape(rows_y, slices, width_x)


def reference(activity, histo_counts, background, blur_values, band_start):
    def one_view(carry, inputs):
        view_counts, view_background, view_values, view_starts = inputs
        return carry + view_gradient(activity, view_counts, view_background, view_values, view_starts), None

    start_value = jnp.zeros(activity.shape, jnp.float32)
    gradient, _ = lax.scan(one_view, start_value, (histo_counts, background, blur_values, band_start))
    return gradient
```

```python
import functools

import jax
import jax.numpy as jnp
from jax import lax
from jax.experimental import pallas as pl
from jax.experimental.pallas import tpu as pltpu
from jax.sharding import PartitionSpec as P

MESH = pl.DeviceIdType.MESH
PAIR = 2
SLABS = 2


def kernel(
    groups, act_ref, counts_ref, back_ref, values_ref, starts_ref, out_ref,
    acts, edges, edge_own, counts, forward_w, backward_w, partial, pair_in, sums, owner_in, halo_out, halo_in,
    counts_sem, line_send, line_recv, pair_send, pair_recv, edge_send, edge_recv,
    halo_send, halo_recv, part_send, part_recv, sum_send, sum_recv,
):
    part = lax.axis_index("parts")
    view = lax.axis_index("view")
    slab = lax.axis_index("slab")
    members = groups * PAIR
    hi = view // PAIR
    lo = view % PAIR
    other = 1 - lo
    rows, slices, width = act_ref.shape
    views = back_ref.shape[0]
    taps = values_ref.shape[0] // views
    band = values_ref.shape[2]
    group_rows = PAIR * rows

    def at(hi_index, lo_index, slab_index):
        return (part, hi_index * PAIR + lo_index, slab_index)

    def ahead(step):
        return lax.rem(hi + step, groups)

    def behind(step):
        return lax.rem(hi + groups - step, groups)

    barrier = pltpu.get_barrier_semaphore()
    for step in range(members):
        pl.semaphore_signal(
            barrier, inc=1, device_id=(part, lax.rem(view + step, members), 1 - slab), device_id_type=MESH
        )
    for step in range(1, groups):
        pl.semaphore_signal(barrier, inc=1, device_id=at(ahead(step), lo, slab), device_id_type=MESH)
    pl.semaphore_signal(barrier, inc=1, device_id=at(hi, other, slab), device_id_type=MESH)

    def counts_copy(step):
        first = pl.multiple_of(behind(step) * group_rows, group_rows)
        return pltpu.make_async_copy(
            counts_ref.at[:, pl.ds(first, group_rows)], counts.at[step], counts_sem.at[step]
        )

    for step in range(groups):
        counts_copy(step).start()

    own = act_ref[...]
    own_wide = own.astype(jnp.float32)
    edge_own[...] = jnp.where(slab == 0, own_wide[:, slices - 1, :], own_wide[:, 0, :]).astype(jnp.bfloat16)
    acts[view] = own

    lane = lax.broadcasted_iota(jnp.int32, (width, 128), 1)

    def build(which):
        line = jnp.broadcast_to(starts_ref[which : which + 1, :].astype(jnp.float32), (128, width))
        start = line.T.astype(jnp.int32)
        turned = jnp.concatenate(
            [values_ref[which].astype(jnp.float32), jnp.zeros((width, 128 - band), jnp.float32)], axis=1
        )
        shift = 1
        while shift < 128:
            turned = jnp.where((start & shift) != 0, pltpu.roll(turned, shift, axis=1), turned)
            shift *= 2
        pieces = []
        for first in range(0, width, 128):
            distance = lane + first - start
            pieces.append(jnp.where((distance >= 0) & (distance < band), turned, 0.0))
        matrix = jnp.concatenate(pieces, axis=1)
        view_index, tap = which // taps, which % taps
        backward_w[view_index * width : (view_index + 1) * width, tap * width : (tap + 1) * width] = (
            matrix.astype(jnp.bfloat16)
        )
        forward_w[tap * width : (tap + 1) * width, view_index * width : (view_index + 1) * width] = (
            matrix.T.astype(jnp.bfloat16)
        )

    total = views * taps
    for which in range(total // 2):
        build(which)

    pl.semaphore_wait(barrier, members + groups)

    def pair_copy(step, source):
        return pltpu.make_async_remote_copy(
            src_ref=source, dst_ref=acts.at[behind(step) * PAIR + lo],
            send_sem=pair_send.at[step], recv_sem=pair_recv.at[step],
            device_id=at(hi, other, slab), device_id_type=MESH,
        )

    def line_copy(step):
        return pltpu.make_async_remote_copy(
            src_ref=act_ref, dst_ref=acts.at[view],
            send_sem=line_send.at[step], recv_sem=line_recv.at[step],
            device_id=at(ahead(step), lo, slab), device_id_type=MESH,
        )

    def edge_copy(step):
        return pltpu.make_async_remote_copy(
            src_ref=edge_own, dst_ref=edges.at[view],
            send_sem=edge_send.at[step], recv_sem=edge_recv.at[step],
            device_id=(part, lax.rem(view + step, members), 1 - slab), device_id_type=MESH,
        )

    pair_copy(0, act_ref).start()
    for step in range(1, groups):
        line_copy(step).start()
    for step in range(members):
        edge_copy(step).start()

    for which in range(total // 2, total):
        build(which)

    for step in range(members):
        edge_copy(step).wait_recv()

    slice_at = lax.broadcasted_iota(jnp.int32, (group_rows, slices, width), 1)
    inner = jnp.where(slab == 0, slices - 1, 0)

    def halo_copy(step):
        return pltpu.make_async_remote_copy(
            src_ref=halo_out.at[step], dst_ref=halo_in.at[step],
            send_sem=halo_send.at[step], recv_sem=halo_recv.at[step],
            device_id=at(hi, lo, 1 - slab), device_id_type=MESH,
        )

    def part_copy(step):
        return pltpu.make_async_remote_copy(
            src_ref=partial.at[step, other], dst_ref=pair_in.at[step],
            send_sem=part_send.at[step], recv_sem=part_recv.at[step],
            device_id=at(hi, other, slab), device_id_type=MESH,
        )

    def sum_copy(step):
        return pltpu.make_async_remote_copy(
            src_ref=sums.at[step], dst_ref=owner_in.at[step],
            send_sem=sum_send.at[step], recv_sem=sum_recv.at[step],
            device_id=at(behind(step), lo, slab), device_id_type=MESH,
        )

    def relay(step):
        line_copy(step).wait_recv()
        pair_copy(step, acts.at[behind(step) * PAIR + lo]).start()

    def reduce_pair(step):
        part_copy(step).wait_recv()
        sums[step] = partial[step, lo] + pair_in[step]

    def one_group(step, carry):
        @pl.when(step + 1 < groups)
        def _():
            relay(step + 1)

        group = behind(step)
        pair_copy(step, act_ref).wait_recv()
        image = acts[pl.ds(group * PAIR, PAIR)].astype(jnp.float32).reshape(group_rows, slices, width)
        edge = edges[pl.ds(group * PAIR, PAIR)].astype(jnp.float32).reshape(group_rows, 1, width)
        lower = jnp.where(slice_at == 0, jnp.where(slab == 0, 0.0, edge), pltpu.roll(image, 1, axis=1))
        upper = jnp.where(
            slice_at == slices - 1, jnp.where(slab == 0, edge, 0.0), pltpu.roll(image, slices - 1, axis=1)
        )
        stacked = jnp.concatenate(
            [x.reshape(-1, width).astype(jnp.bfloat16) for x in (lower, image, upper)], axis=1
        )
        summed = jnp.dot(stacked, forward_w[...], preferred_element_type=jnp.float32)
        counts_copy(step).wait()
        ratios = []
        ratio_edges = []
        for view_index in range(views):
            expected = (
                summed[:, view_index * width : (view_index + 1) * width].reshape(group_rows, slices, width)
                + back_ref[view_index].astype(jnp.float32)[None]
            )
            ratio = counts[step, view_index].astype(jnp.float32) / expected - 1.0
            ratio_edges.append(
                jnp.where(slab == 0, ratio[:, slices - 1, :], ratio[:, 0, :]).astype(jnp.bfloat16)
            )
            ratios.append(ratio.reshape(-1, width).astype(jnp.bfloat16))
        outer = pl.multiple_of((1 - slab) * ((taps - 1) * width), width)
        halo_out[step] = jnp.dot(
            jnp.concatenate(ratio_edges, axis=1), backward_w[:, pl.ds(outer, width)],
            preferred_element_type=jnp.float32,
        )
        halo_copy(step).start()
        spread = jnp.dot(
            jnp.concatenate(ratios, axis=1), backward_w[...], preferred_element_type=jnp.float32
        ).reshape(group_rows, slices, taps * width)
        from_upper = pltpu.roll(spread[:, :, :width], slices - 1, axis=1)
        from_lower = pltpu.roll(spread[:, :, 2 * width :], 1, axis=1)
        halo_copy(step).wait_recv()
        halo = halo_in[step].reshape(group_rows, 1, width)
        from_upper = jnp.where(slice_at == slices - 1, jnp.where(slab == 0, halo, 0.0), from_upper)
        from_lower = jnp.where(slice_at == 0, jnp.where(slab == 0, 0.0, halo), from_lower)
        partial[step] = (spread[:, :, width : 2 * width] + from_upper + from_lower).reshape(
            PAIR, rows, slices, width
        )
        part_copy(step).start()

        @pl.when(step > 0)
        def _():
            reduce_pair(step - 1)

        @pl.when(step > 1)
        def _():
            sum_copy(step - 1).start()

        return carry

    lax.fori_loop(0, groups, one_group, 0)
    reduce_pair(groups - 1)
    if groups > 1:
        sum_copy(groups - 1).start()
    gradient = sums[0]
    for step in range(1, groups):
        sum_copy(step).wait_recv()
        gradient = gradient + owner_in[step]
    out_ref[...] = gradient

    for step in range(1, groups):
        line_copy(step).wait_send()
        sum_copy(step).wait_send()
    for step in range(groups):
        pair_copy(step, act_ref).wait_send()
        halo_copy(step).wait_send()
        part_copy(step).wait_send()
    for step in range(members):
        edge_copy(step).wait_send()


def per_device(activity, histo_counts, background, blur_values, band_start):
    members = lax.axis_size("view")
    groups = members // PAIR
    rows, slices, width = activity.shape
    views, taps, _, band = blur_values.shape
    group_rows = PAIR * rows
    dma = pltpu.SemaphoreType.DMA
    block = (rows, slices, width)
    vmem = pl.BlockSpec(memory_space=pltpu.VMEM)
    return pl.pallas_call(
        functools.partial(kernel, groups),
        out_shape=jax.ShapeDtypeStruct(block, jnp.float32),
        in_specs=[vmem, pl.BlockSpec(memory_space=pl.ANY), vmem, vmem, vmem],
        out_specs=vmem,
        scratch_shapes=[
            pltpu.VMEM((members,) + block, jnp.bfloat16),
            pltpu.VMEM((members, rows, width), jnp.bfloat16),
            pltpu.VMEM((rows, width), jnp.bfloat16),
            pltpu.VMEM((groups, views, group_rows, slices, width), jnp.int32),
            pltpu.VMEM((taps * width, views * width), jnp.bfloat16),
            pltpu.VMEM((views * width, taps * width), jnp.bfloat16),
            pltpu.VMEM((groups, PAIR) + block, jnp.float32),
            pltpu.VMEM((groups,) + block, jnp.float32),
            pltpu.VMEM((groups,) + block, jnp.float32),
            pltpu.VMEM((groups,) + block, jnp.float32),
            pltpu.VMEM((groups, group_rows, width), jnp.float32),
            pltpu.VMEM((groups, group_rows, width), jnp.float32),
            dma((groups,)),
            dma((groups,)), dma((groups,)),
            dma((groups,)), dma((groups,)),
            dma((members,)), dma((members,)),
            dma((groups,)), dma((groups,)),
            dma((groups,)), dma((groups,)),
            dma((groups,)), dma((groups,)),
        ],
        compiler_params=pltpu.CompilerParams(collective_id=0, has_side_effects=True, vmem_limit_bytes=60 << 20),
        name="poisson_gradient",
    )(
        activity, histo_counts, background,
        blur_values.reshape(views * taps, width, band), band_start.reshape(views * taps, width),
    )


def solution(mesh):
    placed = (
        P(("parts", "view"), "slab", None),
        P(("parts", "view"), None, "slab", None),
        P(("parts", "view"), "slab", None),
        P("view", None, None, None),
        P("view", None, None),
    )
    return jax.shard_map(
        per_device,
        mesh=mesh,
        in_specs=placed,
        out_specs=P(("parts", "view"), "slab", None),
        check_vma=False,
    )
```

```python
import functools

import jax
import jax.numpy as jnp
from jax import lax
from jax.experimental import pallas as pl
from jax.experimental.pallas import tpu as pltpu
from jax.sharding import PartitionSpec as P

MESH = pl.DeviceIdType.MESH
PAIR = 2
SLABS = 2


def kernel(
    groups, act_ref, counts_ref, back_ref, values_ref, starts_ref, out_ref,
    acts, edges, edge_own, counts, forward_w, backward_w, partial, pair_in, sums, owner_in, halo_out, halo_in,
    counts_sem, line_send, line_recv, pair_send, pair_recv, edge_send, edge_recv,
    halo_send, halo_recv, part_send, part_recv, sum_send, sum_recv,
):
    part = lax.axis_index("parts")
    view = lax.axis_index("view")
    slab = lax.axis_index("slab")
    members = groups * PAIR
    hi = view // PAIR
    lo = view % PAIR
    other = 1 - lo
    rows, slices, width = act_ref.shape
    views = back_ref.shape[0]
    taps = values_ref.shape[0] // views
    group_rows = PAIR * rows

    def at(hi_index, lo_index, slab_index):
        return (part, hi_index * PAIR + lo_index, slab_index)

    def met(step):
        index, unit = 0, 1
        while unit < groups:
            index += ((hi // unit + step // unit) % 2) * unit
            unit *= 2
        return index

    barrier = pltpu.get_barrier_semaphore()
    for step in range(members):
        pl.semaphore_signal(
            barrier, inc=1, device_id=(part, lax.rem(view + step, members), 1 - slab), device_id_type=MESH
        )
    for step in range(1, groups):
        pl.semaphore_signal(barrier, inc=1, device_id=at(met(step), lo, slab), device_id_type=MESH)
    pl.semaphore_signal(barrier, inc=1, device_id=at(hi, other, slab), device_id_type=MESH)

    def counts_copy(step):
        first = pl.multiple_of(met(step) * group_rows, group_rows)
        return pltpu.make_async_copy(
            counts_ref.at[:, pl.ds(first, group_rows)], counts.at[step], counts_sem.at[step]
        )

    for step in range(groups):
        counts_copy(step).start()

    own = act_ref[...]
    own_wide = own.astype(jnp.float32)
    edge_own[...] = jnp.where(slab == 0, own_wide[:, slices - 1, :], own_wide[:, 0, :]).astype(jnp.bfloat16)
    acts[view] = own

    def build(which):
        view_index, tap = which // taps, which % taps
        start = starts_ref[tap, view_index : view_index + 1, :]
        turned = jnp.concatenate(
            [values_ref[which].astype(jnp.float32), jnp.zeros((8, width), jnp.float32)], axis=0
        )
        shift = 1
        while shift < 8:
            turned = jnp.where((start & shift) != 0, pltpu.roll(turned, shift, axis=0), turned)
            shift *= 2
        while shift < width:
            extra = min(shift, width - turned.shape[0])
            plain = jnp.concatenate([turned, jnp.zeros((extra, width), jnp.float32)], axis=0)
            moved = jnp.concatenate([jnp.zeros((shift, width), jnp.float32), turned], axis=0)[: plain.shape[0]]
            turned = jnp.where((start & shift) != 0, moved, plain)
            shift *= 2
        forward_w[tap * width : (tap + 1) * width, view_index * width : (view_index + 1) * width] = (
            turned.astype(jnp.bfloat16)
        )
        backward_w[view_index * width : (view_index + 1) * width, tap * width : (tap + 1) * width] = (
            turned.T.astype(jnp.bfloat16)
        )

    total = views * taps
    for which in range(total):
        build(which)

    pl.semaphore_wait(barrier, members + groups)

    def pair_copy(step, source):
        return pltpu.make_async_remote_copy(
            src_ref=source, dst_ref=acts.at[met(step) * PAIR + lo],
            send_sem=pair_send.at[step], recv_sem=pair_recv.at[step],
            device_id=at(hi, other, slab), device_id_type=MESH,
        )

    def line_copy(step):
        return pltpu.make_async_remote_copy(
            src_ref=act_ref, dst_ref=acts.at[view],
            send_sem=line_send.at[step], recv_sem=line_recv.at[step],
            device_id=at(met(step), lo, slab), device_id_type=MESH,
        )

    def edge_copy(step):
        return pltpu.make_async_remote_copy(
            src_ref=edge_own, dst_ref=edges.at[view],
            send_sem=edge_send.at[step], recv_sem=edge_recv.at[step],
            device_id=at(met(step // PAIR), (lo + step % PAIR) % PAIR, 1 - slab), device_id_type=MESH,
        )

    for step in range(members):
        edge_copy(step).start()
    pair_copy(0, act_ref).start()
    for step in range(1, groups):
        line_copy(step).start()

    slice_at = lax.broadcasted_iota(jnp.int32, (group_rows, slices, width), 1)
    inner = jnp.where(slab == 0, slices - 1, 0)

    def halo_copy(step):
        return pltpu.make_async_remote_copy(
            src_ref=halo_out.at[step], dst_ref=halo_in.at[step],
            send_sem=halo_send.at[step], recv_sem=halo_recv.at[step],
            device_id=at(hi, lo, 1 - slab), device_id_type=MESH,
        )

    def part_copy(step):
        return pltpu.make_async_remote_copy(
            src_ref=partial.at[step, other], dst_ref=pair_in.at[step],
            send_sem=part_send.at[step], recv_sem=part_recv.at[step],
            device_id=at(hi, other, slab), device_id_type=MESH,
        )

    def sum_copy(step):
        return pltpu.make_async_remote_copy(
            src_ref=sums.at[step], dst_ref=owner_in.at[step],
            send_sem=sum_send.at[step], recv_sem=sum_recv.at[step],
            device_id=at(met(step), lo, slab), device_id_type=MESH,
        )

    def relay(step):
        line_copy(step).wait_recv()
        pair_copy(step, acts.at[met(step) * PAIR + lo]).start()

    def reduce_pair(step):
        part_copy(step).wait_recv()
        sums[step] = partial[step, lo] + pair_in[step]

    def one_group(step, carry):
        @pl.when(step + 1 < groups)
        def _():
            relay(step + 1)

        group = met(step)
        for which in range(PAIR):
            edge_copy(step * PAIR + which).wait_recv()
        pair_copy(step, act_ref).wait_recv()
        image = acts[pl.ds(group * PAIR, PAIR)].astype(jnp.float32).reshape(group_rows, slices, width)
        edge = edges[pl.ds(group * PAIR, PAIR)].astype(jnp.float32).reshape(group_rows, 1, width)
        lower = jnp.where(slice_at == 0, jnp.where(slab == 0, 0.0, edge), pltpu.roll(image, 1, axis=1))
        upper = jnp.where(
            slice_at == slices - 1, jnp.where(slab == 0, edge, 0.0), pltpu.roll(image, slices - 1, axis=1)
        )
        stacked = jnp.concatenate(
            [x.reshape(-1, width).astype(jnp.bfloat16) for x in (lower, image, upper)], axis=1
        )
        summed = jnp.dot(stacked, forward_w[...], preferred_element_type=jnp.float32)
        counts_copy(step).wait()
        ratios = []
        ratio_edges = []
        for view_index in range(views):
            expected = (
                summed[:, view_index * width : (view_index + 1) * width].reshape(group_rows, slices, width)
                + back_ref[view_index].astype(jnp.float32)[None]
            )
            ratio = counts[step, view_index].astype(jnp.float32) / expected - 1.0
            ratio_edges.append(
                jnp.where(slab == 0, ratio[:, slices - 1, :], ratio[:, 0, :]).astype(jnp.bfloat16)
            )
            ratios.append(ratio.reshape(-1, width).astype(jnp.bfloat16))
        outer = pl.multiple_of((1 - slab) * ((taps - 1) * width), width)
        halo_out[step] = jnp.dot(
            jnp.concatenate(ratio_edges, axis=1), backward_w[:, pl.ds(outer, width)],
            preferred_element_type=jnp.float32,
        )
        halo_copy(step).start()
        spread = jnp.dot(
            jnp.concatenate(ratios, axis=1), backward_w[...], preferred_element_type=jnp.float32
        ).reshape(group_rows, slices, taps * width)
        from_upper = pltpu.roll(spread[:, :, :width], slices - 1, axis=1)
        from_lower = pltpu.roll(spread[:, :, 2 * width :], 1, axis=1)
        halo_copy(step).wait_recv()
        halo = halo_in[step].reshape(group_rows, 1, width)
        from_upper = jnp.where(slice_at == slices - 1, jnp.where(slab == 0, halo, 0.0), from_upper)
        from_lower = jnp.where(slice_at == 0, jnp.where(slab == 0, 0.0, halo), from_lower)
        partial[step] = (spread[:, :, width : 2 * width] + from_upper + from_lower).reshape(
            PAIR, rows, slices, width
        )
        part_copy(step).start()

        @pl.when(step > 0)
        def _():
            reduce_pair(step - 1)

        @pl.when(step > 1)
        def _():
            sum_copy(step - 1).start()

        return carry

    lax.fori_loop(0, groups, one_group, 0)
    reduce_pair(groups - 1)
    if groups > 1:
        sum_copy(groups - 1).start()
    gradient = sums[0]
    for step in range(1, groups):
        sum_copy(step).wait_recv()
        gradient = gradient + owner_in[step]
    out_ref[...] = gradient

    for step in range(1, groups):
        line_copy(step).wait_send()
        sum_copy(step).wait_send()
    for step in range(groups):
        pair_copy(step, act_ref).wait_send()
        halo_copy(step).wait_send()
        part_copy(step).wait_send()
    for step in range(members):
        edge_copy(step).wait_send()


def per_device(activity, histo_counts, background, blur_values, band_start):
    members = lax.axis_size("view")
    groups = members // PAIR
    rows, slices, width = activity.shape
    views, taps, _, band = blur_values.shape
    group_rows = PAIR * rows
    dma = pltpu.SemaphoreType.DMA
    block = (rows, slices, width)
    vmem = pl.BlockSpec(memory_space=pltpu.VMEM)
    return pl.pallas_call(
        functools.partial(kernel, groups),
        out_shape=jax.ShapeDtypeStruct(block, jnp.float32),
        in_specs=[vmem, pl.BlockSpec(memory_space=pltpu.HBM), vmem, vmem, vmem],
        out_specs=vmem,
        scratch_shapes=[
            pltpu.VMEM((members,) + block, jnp.bfloat16),
            pltpu.VMEM((members, rows, width), jnp.bfloat16),
            pltpu.VMEM((rows, width), jnp.bfloat16),
            pltpu.VMEM((groups, views, group_rows, slices, width), jnp.int32),
            pltpu.VMEM((taps * width, views * width), jnp.bfloat16),
            pltpu.VMEM((views * width, taps * width), jnp.bfloat16),
            pltpu.VMEM((groups, PAIR) + block, jnp.float32),
            pltpu.VMEM((groups,) + block, jnp.float32),
            pltpu.VMEM((groups,) + block, jnp.float32),
            pltpu.VMEM((groups,) + block, jnp.float32),
            pltpu.VMEM((groups, group_rows, width), jnp.float32),
            pltpu.VMEM((groups, group_rows, width), jnp.float32),
            dma((groups,)),
            dma((groups,)), dma((groups,)),
            dma((groups,)), dma((groups,)),
            dma((members,)), dma((members,)),
            dma((groups,)), dma((groups,)),
            dma((groups,)), dma((groups,)),
            dma((groups,)), dma((groups,)),
        ],
        compiler_params=pltpu.CompilerParams(collective_id=0, has_side_effects=True, vmem_limit_bytes=36 << 20),
        name="poisson_gradient",
    )(
        activity, histo_counts, background,
        jnp.swapaxes(blur_values, 2, 3).reshape(views * taps, band, width), jnp.swapaxes(band_start, 0, 1),
    )


def solution(mesh):
    placed = (
        P(("parts", "view"), "slab", None),
        P(("parts", "view"), None, "slab", None),
        P(("parts", "view"), "slab", None),
        P("view", None, None, None),
        P("view", None, None),
    )
    return jax.shard_map(
        per_device,
        mesh=mesh,
        in_specs=placed,
        out_specs=P(("parts", "view"), "slab", None),
        check_vma=False,
    )
```

```python
import functools

import jax
import jax.numpy as jnp
from jax import lax
from jax.experimental import pallas as pl
from jax.experimental.pallas import tpu as pltpu
from jax.sharding import PartitionSpec as P

MESH = pl.DeviceIdType.MESH
PAIR = 2
SLABS = 2


CODE_MAX = 32767.0
TINY = 1e-30
VMEM_LIMIT = 63 << 20


def encode(block):
    top = jnp.max(jnp.abs(block), axis=(0, 1), keepdims=False)[None, :]
    scale = jnp.where(top > TINY, CODE_MAX / jnp.maximum(top, TINY), 0.0)
    code = jnp.round(block * scale[None]).astype(jnp.int32).astype(jnp.int16)
    return code, jnp.broadcast_to(top * (1.0 / CODE_MAX), (8, block.shape[2]))


def decode(code, unit):
    return code.astype(jnp.int32).astype(jnp.float32) * unit[None, 0:1, :]


def kernel(
    groups, act_hbm, counts_ref, back_hbm, values_hbm, starts_hbm, out_ref,
    act_ref, back_ref, values_ref, starts_ref,
    acts, edges, edge_own, counts, forward_w, backward_w, kept, part_code, part_unit, pair_code, pair_unit, sum_code, sum_unit, owner_code, owner_unit, halo_out, halo_in,
    load_sem, counts_sem, line_send, line_recv, pair_send, pair_recv, edge_send, edge_recv,
    halo_send, halo_recv, part_send, part_recv, sum_send, sum_recv, part_unit_send, part_unit_recv, sum_unit_send, sum_unit_recv,
):
    part = lax.axis_index("parts")
    view = lax.axis_index("view")
    slab = lax.axis_index("slab")
    members = groups * PAIR
    hi = view // PAIR
    lo = view % PAIR
    other = 1 - lo
    rows, slices, width = act_ref.shape
    views = back_ref.shape[0]
    taps = values_ref.shape[0] // views
    group_rows = PAIR * rows

    def at(hi_index, lo_index, slab_index):
        return (part, hi_index * PAIR + lo_index, slab_index)

    def met(step):
        index, unit = 0, 1
        while unit < groups:
            index += ((hi // unit + step // unit) % 2) * unit
            unit *= 2
        return index

    barrier = pltpu.get_barrier_semaphore()
    for step in range(members):
        pl.semaphore_signal(
            barrier, inc=1, device_id=(part, lax.rem(view + step, members), 1 - slab), device_id_type=MESH
        )
    for step in range(1, groups):
        pl.semaphore_signal(barrier, inc=1, device_id=at(met(step), lo, slab), device_id_type=MESH)
    pl.semaphore_signal(barrier, inc=1, device_id=at(hi, other, slab), device_id_type=MESH)

    def counts_copy(step):
        first = pl.multiple_of(met(step) * group_rows, group_rows)
        return pltpu.make_async_copy(
            counts_ref.at[:, pl.ds(first, group_rows)], counts.at[step], counts_sem.at[step]
        )

    loads = [
        pltpu.make_async_copy(source, target, load_sem.at[index])
        for index, (source, target) in enumerate(
            ((values_hbm, values_ref), (starts_hbm, starts_ref), (act_hbm, act_ref), (back_hbm, back_ref))
        )
    ]
    for load in loads:
        load.start()
    for step in range(groups):
        counts_copy(step).start()
    for load in loads:
        load.wait()
    own = act_ref[...]
    own_wide = own.astype(jnp.float32)
    edge_own[...] = jnp.where(slab == 0, own_wide[:, slices - 1, :], own_wide[:, 0, :]).astype(jnp.bfloat16)
    acts[view] = own

    def build(which):
        view_index, tap = which // taps, which % taps
        start = starts_ref[tap, view_index : view_index + 1, :]
        turned = jnp.concatenate(
            [values_ref[which].astype(jnp.float32), jnp.zeros((8, width), jnp.float32)], axis=0
        )
        shift = 1
        while shift < 8:
            turned = jnp.where((start & shift) != 0, pltpu.roll(turned, shift, axis=0), turned)
            shift *= 2
        while shift < width:
            extra = min(shift, width - turned.shape[0])
            plain = jnp.concatenate([turned, jnp.zeros((extra, width), jnp.float32)], axis=0)
            moved = jnp.concatenate([jnp.zeros((shift, width), jnp.float32), turned], axis=0)[: plain.shape[0]]
            turned = jnp.where((start & shift) != 0, moved, plain)
            shift *= 2
        forward_w[tap * width : (tap + 1) * width, view_index * width : (view_index + 1) * width] = (
            turned.astype(jnp.bfloat16)
        )
        backward_w[view_index * width : (view_index + 1) * width, tap * width : (tap + 1) * width] = (
            turned.T.astype(jnp.bfloat16)
        )

    total = views * taps
    for which in range(total):
        build(which)

    pl.semaphore_wait(barrier, members + groups)

    def pair_copy(step, source):
        return pltpu.make_async_remote_copy(
            src_ref=source, dst_ref=acts.at[met(step) * PAIR + lo],
            send_sem=pair_send.at[step], recv_sem=pair_recv.at[step],
            device_id=at(hi, other, slab), device_id_type=MESH,
        )

    def line_copy(step):
        return pltpu.make_async_remote_copy(
            src_ref=act_ref, dst_ref=acts.at[view],
            send_sem=line_send.at[step], recv_sem=line_recv.at[step],
            device_id=at(met(step), lo, slab), device_id_type=MESH,
        )

    def edge_copy(step):
        return pltpu.make_async_remote_copy(
            src_ref=edge_own, dst_ref=edges.at[view],
            send_sem=edge_send.at[step], recv_sem=edge_recv.at[step],
            device_id=at(met(step // PAIR), (lo + step % PAIR) % PAIR, 1 - slab), device_id_type=MESH,
        )

    for step in range(members):
        edge_copy(step).start()
    pair_copy(0, act_ref).start()
    for step in range(1, groups):
        line_copy(step).start()

    slice_at = lax.broadcasted_iota(jnp.int32, (group_rows, slices, width), 1)
    inner = jnp.where(slab == 0, slices - 1, 0)

    def halo_copy(step):
        return pltpu.make_async_remote_copy(
            src_ref=halo_out.at[step], dst_ref=halo_in.at[step],
            send_sem=halo_send.at[step], recv_sem=halo_recv.at[step],
            device_id=at(hi, lo, 1 - slab), device_id_type=MESH,
        )

    def part_copies(step):
        return [
            pltpu.make_async_remote_copy(
                src_ref=source.at[step], dst_ref=target.at[step],
                send_sem=send.at[step], recv_sem=recv.at[step],
                device_id=at(hi, other, slab), device_id_type=MESH,
            )
            for source, target, send, recv in (
                (part_unit, pair_unit, part_unit_send, part_unit_recv),
                (part_code, pair_code, part_send, part_recv),
            )
        ]

    def sum_copies(step):
        return [
            pltpu.make_async_remote_copy(
                src_ref=source.at[step], dst_ref=target.at[step],
                send_sem=send.at[step], recv_sem=recv.at[step],
                device_id=at(met(step), lo, slab), device_id_type=MESH,
            )
            for source, target, send, recv in (
                (sum_unit, owner_unit, sum_unit_send, sum_unit_recv),
                (sum_code, owner_code, sum_send, sum_recv),
            )
        ]

    def relay(step):
        line_copy(step).wait_recv()
        pair_copy(step, acts.at[met(step) * PAIR + lo]).start()

    def pair_sum(step):
        for copy in part_copies(step):
            copy.wait_recv()
        return kept[step] + decode(pair_code[step], pair_unit[step])

    def pass_on(step):
        sum_code[step], sum_unit[step] = encode(pair_sum(step))
        for copy in sum_copies(step):
            copy.start()

    def one_group(step, carry):
        @pl.when(step + 1 < groups)
        def _():
            relay(step + 1)

        group = met(step)
        for which in range(PAIR):
            edge_copy(step * PAIR + which).wait_recv()
        pair_copy(step, act_ref).wait_recv()
        image = acts[pl.ds(group * PAIR, PAIR)].astype(jnp.float32).reshape(group_rows, slices, width)
        edge = edges[pl.ds(group * PAIR, PAIR)].astype(jnp.float32).reshape(group_rows, 1, width)
        lower = jnp.where(slice_at == 0, jnp.where(slab == 0, 0.0, edge), pltpu.roll(image, 1, axis=1))
        upper = jnp.where(
            slice_at == slices - 1, jnp.where(slab == 0, edge, 0.0), pltpu.roll(image, slices - 1, axis=1)
        )
        stacked = jnp.concatenate(
            [x.reshape(-1, width).astype(jnp.bfloat16) for x in (lower, image, upper)], axis=1
        )
        summed = jnp.dot(stacked, forward_w[...], preferred_element_type=jnp.float32)
        counts_copy(step).wait()
        ratios = []
        ratio_edges = []
        for view_index in range(views):
            expected = (
                summed[:, view_index * width : (view_index + 1) * width].reshape(group_rows, slices, width)
                + back_ref[view_index].astype(jnp.float32)[None]
            )
            ratio = counts[step, view_index].astype(jnp.float32) / expected - 1.0
            ratio_edges.append(
                jnp.where(slab == 0, ratio[:, slices - 1, :], ratio[:, 0, :]).astype(jnp.bfloat16)
            )
            ratios.append(ratio.reshape(-1, width).astype(jnp.bfloat16))
        outer = pl.multiple_of((1 - slab) * ((taps - 1) * width), width)
        halo_out[step] = jnp.dot(
            jnp.concatenate(ratio_edges, axis=1), backward_w[:, pl.ds(outer, width)],
            preferred_element_type=jnp.float32,
        )
        halo_copy(step).start()
        spread = jnp.dot(
            jnp.concatenate(ratios, axis=1), backward_w[...], preferred_element_type=jnp.float32
        ).reshape(group_rows, slices, taps * width)
        from_upper = pltpu.roll(spread[:, :, :width], slices - 1, axis=1)
        from_lower = pltpu.roll(spread[:, :, 2 * width :], 1, axis=1)
        halo_copy(step).wait_recv()
        halo = halo_in[step].reshape(group_rows, 1, width)
        from_upper = jnp.where(slice_at == slices - 1, jnp.where(slab == 0, halo, 0.0), from_upper)
        from_lower = jnp.where(slice_at == 0, jnp.where(slab == 0, 0.0, halo), from_lower)
        spread_sum = (spread[:, :, width : 2 * width] + from_upper + from_lower).reshape(
            PAIR, rows, slices, width
        )
        kept[step] = jnp.where(lo == 0, spread_sum[0], spread_sum[1])
        part_code[step], part_unit[step] = encode(jnp.where(lo == 0, spread_sum[1], spread_sum[0]))
        for copy in part_copies(step):
            copy.start()

        @pl.when(step > 1)
        def _():
            pass_on(step - 1)

        return carry

    lax.fori_loop(0, groups, one_group, 0)
    if groups > 1:
        pass_on(groups - 1)
    gradient = pair_sum(0)
    for step in range(1, groups):
        for copy in sum_copies(step):
            copy.wait_recv()
        gradient = gradient + decode(owner_code[step], owner_unit[step])
    out_ref[...] = gradient

    for step in range(1, groups):
        line_copy(step).wait_send()
        for copy in sum_copies(step):
            copy.wait_send()
    for step in range(groups):
        pair_copy(step, act_ref).wait_send()
        halo_copy(step).wait_send()
        for copy in part_copies(step):
            copy.wait_send()
    for step in range(members):
        edge_copy(step).wait_send()


def per_device(activity, histo_counts, background, blur_values, band_start):
    members = lax.axis_size("view")
    groups = members // PAIR
    rows, slices, width = activity.shape
    views, taps, _, band = blur_values.shape
    group_rows = PAIR * rows
    dma = pltpu.SemaphoreType.DMA
    block = (rows, slices, width)
    vmem = pl.BlockSpec(memory_space=pltpu.VMEM)
    return pl.pallas_call(
        functools.partial(kernel, groups),
        out_shape=jax.ShapeDtypeStruct(block, jnp.float32),
        in_specs=[pl.BlockSpec(memory_space=pl.ANY)] * 5,
        out_specs=vmem,
        scratch_shapes=[
            pltpu.VMEM(block, jnp.bfloat16),
            pltpu.VMEM(background.shape, jnp.bfloat16),
            pltpu.VMEM((views * taps, band, width), jnp.bfloat16),
            pltpu.VMEM((taps, views, width), jnp.int32),
            pltpu.VMEM((members,) + block, jnp.bfloat16),
            pltpu.VMEM((members, rows, width), jnp.bfloat16),
            pltpu.VMEM((rows, width), jnp.bfloat16),
            pltpu.VMEM((groups, views, group_rows, slices, width), jnp.int32),
            pltpu.VMEM((taps * width, views * width), jnp.bfloat16),
            pltpu.VMEM((views * width, taps * width), jnp.bfloat16),
            pltpu.VMEM((groups,) + block, jnp.float32),
            pltpu.VMEM((groups,) + block, jnp.int16),
            pltpu.VMEM((groups, 8, width), jnp.float32),
            pltpu.VMEM((groups,) + block, jnp.int16),
            pltpu.VMEM((groups, 8, width), jnp.float32),
            pltpu.VMEM((groups,) + block, jnp.int16),
            pltpu.VMEM((groups, 8, width), jnp.float32),
            pltpu.VMEM((groups,) + block, jnp.int16),
            pltpu.VMEM((groups, 8, width), jnp.float32),
            pltpu.VMEM((groups, group_rows, width), jnp.float32),
            pltpu.VMEM((groups, group_rows, width), jnp.float32),
            dma((4,)),
            dma((groups,)),
            dma((groups,)), dma((groups,)),
            dma((groups,)), dma((groups,)),
            dma((members,)), dma((members,)),
            dma((groups,)), dma((groups,)),
            dma((groups,)), dma((groups,)),
            dma((groups,)), dma((groups,)),
            dma((groups,)), dma((groups,)),
            dma((groups,)), dma((groups,)),
        ],
        compiler_params=pltpu.CompilerParams(collective_id=0, has_side_effects=True, vmem_limit_bytes=VMEM_LIMIT),
        name="poisson_gradient",
    )(
        activity, histo_counts, background,
        jnp.swapaxes(blur_values, 2, 3).reshape(views * taps, band, width), jnp.swapaxes(band_start, 0, 1),
    )


def solution(mesh):
    placed = (
        P(("parts", "view"), "slab", None),
        P(("parts", "view"), None, "slab", None),
        P(("parts", "view"), "slab", None),
        P("view", None, None, None),
        P("view", None, None),
    )
    return jax.shard_map(
        per_device,
        mesh=mesh,
        in_specs=placed,
        out_specs=P(("parts", "view"), "slab", None),
        check_vma=False,
    )
```

```python
import functools

import jax
import jax.numpy as jnp
from jax import lax
from jax.experimental import pallas as pl
from jax.experimental.pallas import tpu as pltpu
from jax.sharding import PartitionSpec as P

MESH = pl.DeviceIdType.MESH
PAIR = 2
SLABS = 2


CODE_MAX = 32767.0
TINY = 1e-30
VMEM_LIMIT = 63 << 20


def encode(block):
    top = jnp.max(jnp.abs(block), axis=(0, 1), keepdims=False)[None, :]
    scale = jnp.where(top > TINY, CODE_MAX / jnp.maximum(top, TINY), 0.0)
    code = jnp.round(block * scale[None]).astype(jnp.int32).astype(jnp.int16)
    return code, jnp.broadcast_to(top * (1.0 / CODE_MAX), (8, block.shape[2]))


def decode(code, unit):
    return code.astype(jnp.int32).astype(jnp.float32) * unit[None, 0:1, :]


def kernel(
    groups, act_hbm, counts_ref, back_hbm, values_hbm, starts_hbm, out_ref,
    act_ref, back_ref, values_ref, starts_ref,
    acts, edges, edge_own, counts, forward_w, backward_w, kept, part_code, part_unit, pair_code, pair_unit, sum_code, sum_unit, owner_code, owner_unit, halo_out, halo_in,
    load_sem, counts_sem, line_send, line_recv, pair_send, pair_recv, edge_send, edge_recv,
    halo_send, halo_recv, part_send, part_recv, sum_send, sum_recv, part_unit_send, part_unit_recv, sum_unit_send, sum_unit_recv,
):
    part = lax.axis_index("parts")
    view = lax.axis_index("view")
    slab = lax.axis_index("slab")
    members = groups * PAIR
    last = groups - 1
    hi = view // PAIR
    lo = view % PAIR
    other = 1 - lo
    rows, slices, width = act_ref.shape
    views = back_ref.shape[0]
    taps = values_ref.shape[0] // views
    group_rows = PAIR * rows

    def at(hi_index, lo_index, slab_index):
        return (part, hi_index * PAIR + lo_index, slab_index)

    def met(step):
        key = (groups - step) % groups
        index, unit = 0, 1
        while unit < groups:
            index += ((hi // unit + key // unit) % 2) * unit
            unit *= 2
        return index

    barrier = pltpu.get_barrier_semaphore()
    for step in range(members):
        pl.semaphore_signal(
            barrier, inc=1, device_id=(part, lax.rem(view + step, members), 1 - slab), device_id_type=MESH
        )
    for step in range(1, groups):
        pl.semaphore_signal(barrier, inc=1, device_id=at(met(step), lo, slab), device_id_type=MESH)
    pl.semaphore_signal(barrier, inc=1, device_id=at(hi, other, slab), device_id_type=MESH)
    pl.semaphore_signal(barrier, inc=1, device_id=at(met(last), other, slab), device_id_type=MESH)

    def counts_copy(step):
        first = pl.multiple_of(met(step) * group_rows, group_rows)
        return pltpu.make_async_copy(
            counts_ref.at[:, pl.ds(first, group_rows)], counts.at[step], counts_sem.at[step]
        )

    loads = [
        pltpu.make_async_copy(source, target, load_sem.at[index])
        for index, (source, target) in enumerate(
            ((values_hbm, values_ref), (starts_hbm, starts_ref), (act_hbm, act_ref), (back_hbm, back_ref))
        )
    ]
    for load in loads:
        load.start()
    for step in range(groups):
        counts_copy(step).start()
    for load in loads:
        load.wait()
    own = act_ref[...]
    own_wide = own.astype(jnp.float32)
    edge_own[...] = jnp.where(slab == 0, own_wide[:, slices - 1, :], own_wide[:, 0, :]).astype(jnp.bfloat16)
    acts[view] = own

    def build(which):
        view_index, tap = which // taps, which % taps
        start = starts_ref[tap, view_index : view_index + 1, :]
        turned = jnp.concatenate(
            [values_ref[which].astype(jnp.float32), jnp.zeros((8, width), jnp.float32)], axis=0
        )
        shift = 1
        while shift < 8:
            turned = jnp.where((start & shift) != 0, pltpu.roll(turned, shift, axis=0), turned)
            shift *= 2
        while shift < width:
            extra = min(shift, width - turned.shape[0])
            plain = jnp.concatenate([turned, jnp.zeros((extra, width), jnp.float32)], axis=0)
            moved = jnp.concatenate([jnp.zeros((shift, width), jnp.float32), turned], axis=0)[: plain.shape[0]]
            turned = jnp.where((start & shift) != 0, moved, plain)
            shift *= 2
        forward_w[tap * width : (tap + 1) * width, view_index * width : (view_index + 1) * width] = (
            turned.astype(jnp.bfloat16)
        )
        backward_w[view_index * width : (view_index + 1) * width, tap * width : (tap + 1) * width] = (
            turned.T.astype(jnp.bfloat16)
        )

    total = views * taps
    for which in range(total):
        build(which)

    pl.semaphore_wait(barrier, members + groups + 1)

    def pair_copy(step, source):
        return pltpu.make_async_remote_copy(
            src_ref=source, dst_ref=acts.at[met(step) * PAIR + lo],
            send_sem=pair_send.at[step], recv_sem=pair_recv.at[step],
            device_id=at(hi, other, slab), device_id_type=MESH,
        )

    def near_copy():
        return pltpu.make_async_remote_copy(
            src_ref=acts.at[hi * PAIR + other], dst_ref=acts.at[hi * PAIR + other],
            send_sem=pair_send.at[last], recv_sem=pair_recv.at[last],
            device_id=at(met(last), lo, slab), device_id_type=MESH,
        )

    def line_copy(step):
        return pltpu.make_async_remote_copy(
            src_ref=act_ref, dst_ref=acts.at[view],
            send_sem=line_send.at[step], recv_sem=line_recv.at[step],
            device_id=at(met(step), lo, slab), device_id_type=MESH,
        )

    def edge_copy(step):
        return pltpu.make_async_remote_copy(
            src_ref=edge_own, dst_ref=edges.at[view],
            send_sem=edge_send.at[step], recv_sem=edge_recv.at[step],
            device_id=at(met(step // PAIR), (lo + step % PAIR) % PAIR, 1 - slab), device_id_type=MESH,
        )

    for step in range(members):
        edge_copy(step).start()
    pair_copy(0, act_ref).start()
    for step in range(1, groups):
        line_copy(step).start()

    slice_at = lax.broadcasted_iota(jnp.int32, (group_rows, slices, width), 1)
    inner = jnp.where(slab == 0, slices - 1, 0)

    def halo_copies(step):
        return [
            pltpu.make_async_remote_copy(
                src_ref=halo_out.at[step, keeper], dst_ref=halo_in.at[step, index],
                send_sem=halo_send.at[step, index], recv_sem=halo_recv.at[step, index],
                device_id=at(hi, keeper, 1 - slab), device_id_type=MESH,
            )
            for index, keeper in enumerate((lo, other))
        ]

    def part_copies(step, target):
        return [
            pltpu.make_async_remote_copy(
                src_ref=source.at[step], dst_ref=landing.at[step],
                send_sem=send.at[step], recv_sem=recv.at[step],
                device_id=at(target, other, slab), device_id_type=MESH,
            )
            for source, landing, send, recv in (
                (part_unit, pair_unit, part_unit_send, part_unit_recv),
                (part_code, pair_code, part_send, part_recv),
            )
        ]

    def sum_copies(step):
        return [
            pltpu.make_async_remote_copy(
                src_ref=source.at[step], dst_ref=target.at[step],
                send_sem=send.at[step], recv_sem=recv.at[step],
                device_id=at(met(step), lo, slab), device_id_type=MESH,
            )
            for source, target, send, recv in (
                (sum_unit, owner_unit, sum_unit_send, sum_unit_recv),
                (sum_code, owner_code, sum_send, sum_recv),
            )
        ]

    def relay(step):
        line_copy(step).wait_recv()
        pair_copy(step, acts.at[met(step) * PAIR + lo]).start()

    def kept_sum(step):
        for copy in halo_copies(step):
            copy.wait_recv()
        halo = (halo_in[step, 0] + halo_in[step, 1]).reshape(rows, 1, width)
        return kept[step] + jnp.where(slice_at[:rows] == inner, halo, 0.0)

    def pair_part(step):
        for copy in part_copies(step, hi):
            copy.wait_recv()
        return decode(pair_code[step], pair_unit[step])

    def pass_on(step, value):
        sum_code[step], sum_unit[step] = encode(value)
        for copy in sum_copies(step):
            copy.start()

    def one_group(step, carry):
        group = met(step)
        for which in range(PAIR):
            edge_copy(step * PAIR + which).wait_recv()
        pair_copy(step, act_ref).wait_recv()

        @pl.when(step == 0)
        def _():
            near_copy().start()

        @pl.when(step == last)
        def _():
            line_copy(last).wait_recv()

        image = acts[pl.ds(group * PAIR, PAIR)].astype(jnp.float32).reshape(group_rows, slices, width)
        edge = edges[pl.ds(group * PAIR, PAIR)].astype(jnp.float32).reshape(group_rows, 1, width)
        lower = jnp.where(slice_at == 0, jnp.where(slab == 0, 0.0, edge), pltpu.roll(image, 1, axis=1))
        upper = jnp.where(
            slice_at == slices - 1, jnp.where(slab == 0, edge, 0.0), pltpu.roll(image, slices - 1, axis=1)
        )
        stacked = jnp.concatenate(
            [x.reshape(-1, width).astype(jnp.bfloat16) for x in (lower, image, upper)], axis=1
        )
        summed = jnp.dot(stacked, forward_w[...], preferred_element_type=jnp.float32)
        counts_copy(step).wait()
        ratios = []
        ratio_edges = []
        for view_index in range(views):
            expected = (
                summed[:, view_index * width : (view_index + 1) * width].reshape(group_rows, slices, width)
                + back_ref[view_index].astype(jnp.float32)[None]
            )
            ratio = counts[step, view_index].astype(jnp.float32) / expected - 1.0
            ratio_edges.append(
                jnp.where(slab == 0, ratio[:, slices - 1, :], ratio[:, 0, :]).astype(jnp.bfloat16)
            )
            ratios.append(ratio.reshape(-1, width).astype(jnp.bfloat16))
        outer = pl.multiple_of((1 - slab) * ((taps - 1) * width), width)
        halo_out[step] = jnp.dot(
            jnp.concatenate(ratio_edges, axis=1), backward_w[:, pl.ds(outer, width)],
            preferred_element_type=jnp.float32,
        ).reshape(PAIR, rows, width)
        for copy in halo_copies(step):
            copy.start()
        spread = jnp.dot(
            jnp.concatenate(ratios, axis=1), backward_w[...], preferred_element_type=jnp.float32
        ).reshape(group_rows, slices, taps * width)
        from_upper = pltpu.roll(spread[:, :, :width], slices - 1, axis=1)
        from_lower = pltpu.roll(spread[:, :, 2 * width :], 1, axis=1)
        from_upper = jnp.where(slice_at == slices - 1, 0.0, from_upper)
        from_lower = jnp.where(slice_at == 0, 0.0, from_lower)
        spread_sum = (spread[:, :, width : 2 * width] + from_upper + from_lower).reshape(
            PAIR, rows, slices, width
        )
        kept[step] = jnp.where(lo == 0, spread_sum[0], spread_sum[1])
        part_code[step], part_unit[step] = encode(jnp.where(lo == 0, spread_sum[1], spread_sum[0]))

        @pl.when(step == 0)
        def _():
            for later in range(1, last):
                relay(later)

        @pl.when(step < last)
        def _():
            for copy in part_copies(step, hi):
                copy.start()

        @pl.when(step == last)
        def _():
            for copy in part_copies(step, met(last)):
                copy.start()

        @pl.when(step > 1)
        def _():
            pass_on(step - 1, kept_sum(step - 1) + pair_part(step - 1))

        return carry

    lax.fori_loop(0, groups, one_group, 0)
    pass_on(last, kept_sum(last))
    gradient = kept_sum(0) + pair_part(0)
    for step in range(1, groups):
        for copy in sum_copies(step):
            copy.wait_recv()
        gradient = gradient + decode(owner_code[step], owner_unit[step])
    out_ref[...] = gradient + pair_part(last)

    for step in range(1, groups):
        line_copy(step).wait_send()
        for copy in sum_copies(step):
            copy.wait_send()
    for step in range(groups):
        pair_copy(step, act_ref).wait_send()
        for copy in halo_copies(step):
            copy.wait_send()
        for copy in part_copies(step, hi):
            copy.wait_send()
    for step in range(members):
        edge_copy(step).wait_send()


def per_device(activity, histo_counts, background, blur_values, band_start):
    members = lax.axis_size("view")
    groups = members // PAIR
    rows, slices, width = activity.shape
    views, taps, _, band = blur_values.shape
    group_rows = PAIR * rows
    dma = pltpu.SemaphoreType.DMA
    block = (rows, slices, width)
    vmem = pl.BlockSpec(memory_space=pltpu.VMEM)
    return pl.pallas_call(
        functools.partial(kernel, groups),
        out_shape=jax.ShapeDtypeStruct(block, jnp.float32),
        in_specs=[pl.BlockSpec(memory_space=pl.ANY)] * 5,
        out_specs=vmem,
        scratch_shapes=[
            pltpu.VMEM(block, jnp.bfloat16),
            pltpu.VMEM(background.shape, jnp.bfloat16),
            pltpu.VMEM((views * taps, band, width), jnp.bfloat16),
            pltpu.VMEM((taps, views, width), jnp.int32),
            pltpu.VMEM((members,) + block, jnp.bfloat16),
            pltpu.VMEM((members, rows, width), jnp.bfloat16),
            pltpu.VMEM((rows, width), jnp.bfloat16),
            pltpu.VMEM((groups, views, group_rows, slices, width), jnp.int32),
            pltpu.VMEM((taps * width, views * width), jnp.bfloat16),
            pltpu.VMEM((views * width, taps * width), jnp.bfloat16),
            pltpu.VMEM((groups,) + block, jnp.float32),
            pltpu.VMEM((groups,) + block, jnp.int16),
            pltpu.VMEM((groups, 8, width), jnp.float32),
            pltpu.VMEM((groups,) + block, jnp.int16),
            pltpu.VMEM((groups, 8, width), jnp.float32),
            pltpu.VMEM((groups,) + block, jnp.int16),
            pltpu.VMEM((groups, 8, width), jnp.float32),
            pltpu.VMEM((groups,) + block, jnp.int16),
            pltpu.VMEM((groups, 8, width), jnp.float32),
            pltpu.VMEM((groups, PAIR, rows, width), jnp.float32),
            pltpu.VMEM((groups, PAIR, rows, width), jnp.float32),
            dma((4,)),
            dma((groups,)),
            dma((groups,)), dma((groups,)),
            dma((groups,)), dma((groups,)),
            dma((members,)), dma((members,)),
            dma((groups, PAIR)), dma((groups, PAIR)),
            dma((groups,)), dma((groups,)),
            dma((groups,)), dma((groups,)),
            dma((groups,)), dma((groups,)),
            dma((groups,)), dma((groups,)),
        ],
        compiler_params=pltpu.CompilerParams(collective_id=0, has_side_effects=True, vmem_limit_bytes=VMEM_LIMIT),
        name="poisson_gradient",
    )(
        activity, histo_counts, background,
        jnp.swapaxes(blur_values, 2, 3).reshape(views * taps, band, width), jnp.swapaxes(band_start, 0, 1),
    )


def solution(mesh):
    placed = (
        P(("parts", "view"), "slab", None),
        P(("parts", "view"), None, "slab", None),
        P(("parts", "view"), "slab", None),
        P("view", None, None, None),
        P("view", None, None),
    )
    return jax.shard_map(
        per_device,
        mesh=mesh,
        in_specs=placed,
        out_specs=P(("parts", "view"), "slab", None),
        check_vma=False,
    )
```

```python
import functools

import jax
import jax.numpy as jnp
from jax import lax
from jax.experimental import pallas as pl
from jax.experimental.pallas import tpu as pltpu
from jax.sharding import PartitionSpec as P

MESH = pl.DeviceIdType.MESH
PAIR = 2
SLABS = 2


CODE_MAX = 32767.0
TINY = 1e-30
VMEM_LIMIT = 63 << 20


def encode(block):
    top = jnp.max(jnp.abs(block), axis=(0, 1), keepdims=False)[None, :]
    scale = jnp.where(top > TINY, CODE_MAX / jnp.maximum(top, TINY), 0.0)
    code = jnp.round(block * scale[None]).astype(jnp.int32).astype(jnp.int16)
    return code, jnp.broadcast_to(top * (1.0 / CODE_MAX), (8, block.shape[2]))


def decode(code, unit):
    return code.astype(jnp.int32).astype(jnp.float32) * unit[None, 0:1, :]


def kernel(
    groups, act_hbm, counts_ref, back_hbm, values_hbm, starts_hbm, out_ref,
    act_ref, back_ref, values_ref, starts_ref,
    acts, edges, edge_own, counts, forward_w, backward_w, kept, part_code, part_unit, pair_code, pair_unit, sum_code, sum_unit, owner_code, owner_unit, halo_out, halo_in,
    load_sem, counts_sem, line_send, line_recv, pair_send, pair_recv, edge_send, edge_recv,
    halo_send, halo_recv, part_send, part_recv, sum_send, sum_recv, part_unit_send, part_unit_recv, sum_unit_send, sum_unit_recv,
):
    part = lax.axis_index("parts")
    view = lax.axis_index("view")
    slab = lax.axis_index("slab")
    members = groups * PAIR
    last = groups - 1
    hi = view // PAIR
    lo = view % PAIR
    other = 1 - lo
    rows, slices, width = act_ref.shape
    views = back_ref.shape[0]
    taps = values_ref.shape[0] // views
    group_rows = PAIR * rows

    def at(hi_index, lo_index, slab_index):
        return (part, hi_index * PAIR + lo_index, slab_index)

    def met(step):
        key = (groups - step) % groups
        index, unit = 0, 1
        while unit < groups:
            index += ((hi // unit + key // unit) % 2) * unit
            unit *= 2
        return index

    barrier = pltpu.get_barrier_semaphore()
    for step in range(members):
        pl.semaphore_signal(
            barrier, inc=1, device_id=(part, lax.rem(view + step, members), 1 - slab), device_id_type=MESH
        )
    for step in range(1, groups):
        pl.semaphore_signal(barrier, inc=1, device_id=at(met(step), lo, slab), device_id_type=MESH)
    pl.semaphore_signal(barrier, inc=1, device_id=at(hi, other, slab), device_id_type=MESH)
    pl.semaphore_signal(barrier, inc=1, device_id=at(met(last), other, slab), device_id_type=MESH)

    def counts_copy(step):
        first = pl.multiple_of(met(step) * group_rows, group_rows)
        return pltpu.make_async_copy(
            counts_ref.at[:, pl.ds(first, group_rows)], counts.at[step], counts_sem.at[step]
        )

    loads = [
        pltpu.make_async_copy(source, target, load_sem.at[index])
        for index, (source, target) in enumerate(
            ((values_hbm, values_ref), (starts_hbm, starts_ref), (act_hbm, act_ref), (back_hbm, back_ref))
        )
    ]
    for load in loads:
        load.start()
    for step in range(groups):
        counts_copy(step).start()
    for load in loads:
        load.wait()
    own = act_ref[...]
    own_wide = own.astype(jnp.float32)
    edge_own[...] = jnp.where(slab == 0, own_wide[:, slices - 1, :], own_wide[:, 0, :]).astype(jnp.bfloat16)
    acts[view] = own

    def build(which):
        view_index, tap = which // taps, which % taps
        start = starts_ref[tap, view_index : view_index + 1, :]
        turned = jnp.concatenate(
            [values_ref[which].astype(jnp.float32), jnp.zeros((8, width), jnp.float32)], axis=0
        )
        shift = 1
        while shift < 8:
            turned = jnp.where((start & shift) != 0, pltpu.roll(turned, shift, axis=0), turned)
            shift *= 2
        while shift < width:
            extra = min(shift, width - turned.shape[0])
            plain = jnp.concatenate([turned, jnp.zeros((extra, width), jnp.float32)], axis=0)
            moved = jnp.concatenate([jnp.zeros((shift, width), jnp.float32), turned], axis=0)[: plain.shape[0]]
            turned = jnp.where((start & shift) != 0, moved, plain)
            shift *= 2
        forward_w[tap * width : (tap + 1) * width, view_index * width : (view_index + 1) * width] = (
            turned.astype(jnp.bfloat16)
        )
        backward_w[view_index * width : (view_index + 1) * width, tap * width : (tap + 1) * width] = (
            turned.T.astype(jnp.bfloat16)
        )

    total = views * taps
    for which in range(total):
        build(which)

    pl.semaphore_wait(barrier, members + groups + 1)

    def pair_copy(step, source):
        return pltpu.make_async_remote_copy(
            src_ref=source, dst_ref=acts.at[met(step) * PAIR + lo],
            send_sem=pair_send.at[step], recv_sem=pair_recv.at[step],
            device_id=at(hi, other, slab), device_id_type=MESH,
        )

    def near_copy():
        return pltpu.make_async_remote_copy(
            src_ref=acts.at[hi * PAIR + other], dst_ref=acts.at[hi * PAIR + other],
            send_sem=pair_send.at[last], recv_sem=pair_recv.at[last],
            device_id=at(met(last), lo, slab), device_id_type=MESH,
        )

    def line_copy(step):
        return pltpu.make_async_remote_copy(
            src_ref=act_ref, dst_ref=acts.at[view],
            send_sem=line_send.at[step], recv_sem=line_recv.at[step],
            device_id=at(met(step), lo, slab), device_id_type=MESH,
        )

    def edge_copy(step):
        return pltpu.make_async_remote_copy(
            src_ref=edge_own, dst_ref=edges.at[view],
            send_sem=edge_send.at[step], recv_sem=edge_recv.at[step],
            device_id=at(met(step // PAIR), (lo + step % PAIR) % PAIR, 1 - slab), device_id_type=MESH,
        )

    for step in range(members):
        edge_copy(step).start()
    pair_copy(0, act_ref).start()
    for step in range(1, groups):
        line_copy(step).start()

    slice_at = lax.broadcasted_iota(jnp.int32, (group_rows, slices, width), 1)
    inner = jnp.where(slab == 0, slices - 1, 0)

    def halo_copies(step):
        return [
            pltpu.make_async_remote_copy(
                src_ref=halo_out.at[step, keeper], dst_ref=halo_in.at[step, index],
                send_sem=halo_send.at[step, index], recv_sem=halo_recv.at[step, index],
                device_id=at(hi, keeper, 1 - slab), device_id_type=MESH,
            )
            for index, keeper in enumerate((lo, other))
        ]

    def part_copies(step, target):
        return [
            pltpu.make_async_remote_copy(
                src_ref=source.at[step], dst_ref=landing.at[step],
                send_sem=send.at[step], recv_sem=recv.at[step],
                device_id=at(target, other, slab), device_id_type=MESH,
            )
            for source, landing, send, recv in (
                (part_unit, pair_unit, part_unit_send, part_unit_recv),
                (part_code, pair_code, part_send, part_recv),
            )
        ]

    def sum_copies(step):
        return [
            pltpu.make_async_remote_copy(
                src_ref=source.at[step], dst_ref=target.at[step],
                send_sem=send.at[step], recv_sem=recv.at[step],
                device_id=at(met(step), lo, slab), device_id_type=MESH,
            )
            for source, target, send, recv in (
                (sum_unit, owner_unit, sum_unit_send, sum_unit_recv),
                (sum_code, owner_code, sum_send, sum_recv),
            )
        ]

    def relay(step):
        line_copy(step).wait_recv()
        pair_copy(step, acts.at[met(step) * PAIR + lo]).start()

    def kept_sum(step):
        for copy in halo_copies(step):
            copy.wait_recv()
        halo = (halo_in[step, 0] + halo_in[step, 1]).reshape(rows, 1, width)
        return kept[step] + jnp.where(slice_at[:rows] == inner, halo, 0.0)

    def pair_part(step):
        for copy in part_copies(step, hi):
            copy.wait_recv()
        return decode(pair_code[step], pair_unit[step])

    def pass_on(step, value):
        sum_code[step], sum_unit[step] = encode(value)
        for copy in sum_copies(step):
            copy.start()

    def one_group(step, carry):
        group = met(step)
        for which in range(PAIR):
            edge_copy(step * PAIR + which).wait_recv()
        pair_copy(step, act_ref).wait_recv()

        @pl.when(step == 0)
        def _():
            near_copy().start()

        @pl.when(step == last)
        def _():
            line_copy(last).wait_recv()

        image = acts[pl.ds(group * PAIR, PAIR)].astype(jnp.float32).reshape(group_rows, slices, width)
        edge = edges[pl.ds(group * PAIR, PAIR)].astype(jnp.float32).reshape(group_rows, 1, width)
        lower = jnp.where(slice_at == 0, jnp.where(slab == 0, 0.0, edge), pltpu.roll(image, 1, axis=1))
        upper = jnp.where(
            slice_at == slices - 1, jnp.where(slab == 0, edge, 0.0), pltpu.roll(image, slices - 1, axis=1)
        )
        stacked = jnp.concatenate(
            [x.reshape(-1, width).astype(jnp.bfloat16) for x in (lower, image, upper)], axis=1
        )
        summed = jnp.dot(stacked, forward_w[...], preferred_element_type=jnp.float32)
        counts_copy(step).wait()
        ratios = []
        ratio_edges = []
        for view_index in range(views):
            expected = (
                summed[:, view_index * width : (view_index + 1) * width].reshape(group_rows, slices, width)
                + back_ref[view_index].astype(jnp.float32)[None]
            )
            ratio = counts[step, view_index].astype(jnp.float32) / expected - 1.0
            ratio_edges.append(
                jnp.where(slab == 0, ratio[:, slices - 1, :], ratio[:, 0, :]).astype(jnp.bfloat16)
            )
            ratios.append(ratio.reshape(-1, width).astype(jnp.bfloat16))
        outer = pl.multiple_of((1 - slab) * ((taps - 1) * width), width)
        halo_out[step] = jnp.dot(
            jnp.concatenate(ratio_edges, axis=1), backward_w[:, pl.ds(outer, width)],
            preferred_element_type=jnp.float32,
        ).reshape(PAIR, rows, width)
        for copy in halo_copies(step):
            copy.start()
        spread = jnp.dot(
            jnp.concatenate(ratios, axis=1), backward_w[...], preferred_element_type=jnp.float32
        ).reshape(group_rows, slices, taps * width)
        from_upper = pltpu.roll(spread[:, :, :width], slices - 1, axis=1)
        from_lower = pltpu.roll(spread[:, :, 2 * width :], 1, axis=1)
        from_upper = jnp.where(slice_at == slices - 1, 0.0, from_upper)
        from_lower = jnp.where(slice_at == 0, 0.0, from_lower)
        spread_sum = (spread[:, :, width : 2 * width] + from_upper + from_lower).reshape(
            PAIR, rows, slices, width
        )
        kept[step] = jnp.where(lo == 0, spread_sum[0], spread_sum[1])
        part_code[step], part_unit[step] = encode(jnp.where(lo == 0, spread_sum[1], spread_sum[0]))

        @pl.when(step == 0)
        def _():
            for later in range(1, last):
                relay(later)

        @pl.when(step < last)
        def _():
            for copy in part_copies(step, hi):
                copy.start()

        @pl.when(step == last)
        def _():
            for copy in part_copies(step, met(last)):
                copy.start()

        @pl.when(step > 2)
        def _():
            pass_on(step - 2, kept_sum(step - 2) + pair_part(step - 2))

        return carry

    lax.fori_loop(0, groups, one_group, 0)
    pass_on(last, kept_sum(last))
    if last > 1:
        pass_on(last - 1, kept_sum(last - 1) + pair_part(last - 1))
    gradient = kept_sum(0) + pair_part(0)
    for step in range(1, groups):
        for copy in sum_copies(step):
            copy.wait_recv()
        gradient = gradient + decode(owner_code[step], owner_unit[step])
    out_ref[...] = gradient + pair_part(last)

    for step in range(1, groups):
        line_copy(step).wait_send()
        for copy in sum_copies(step):
            copy.wait_send()
    for step in range(groups):
        pair_copy(step, act_ref).wait_send()
        for copy in halo_copies(step):
            copy.wait_send()
        for copy in part_copies(step, hi):
            copy.wait_send()
    for step in range(members):
        edge_copy(step).wait_send()


def per_device(activity, histo_counts, background, blur_values, band_start):
    members = lax.axis_size("view")
    groups = members // PAIR
    rows, slices, width = activity.shape
    views, taps, _, band = blur_values.shape
    group_rows = PAIR * rows
    dma = pltpu.SemaphoreType.DMA
    block = (rows, slices, width)
    vmem = pl.BlockSpec(memory_space=pltpu.VMEM)
    return pl.pallas_call(
        functools.partial(kernel, groups),
        out_shape=jax.ShapeDtypeStruct(block, jnp.float32),
        in_specs=[pl.BlockSpec(memory_space=pl.ANY)] * 5,
        out_specs=vmem,
        scratch_shapes=[
            pltpu.VMEM(block, jnp.bfloat16),
            pltpu.VMEM(background.shape, jnp.bfloat16),
            pltpu.VMEM((views * taps, band, width), jnp.bfloat16),
            pltpu.VMEM((taps, views, width), jnp.int32),
            pltpu.VMEM((members,) + block, jnp.bfloat16),
            pltpu.VMEM((members, rows, width), jnp.bfloat16),
            pltpu.VMEM((rows, width), jnp.bfloat16),
            pltpu.VMEM((groups, views, group_rows, slices, width), jnp.int32),
            pltpu.VMEM((taps * width, views * width), jnp.bfloat16),
            pltpu.VMEM((views * width, taps * width), jnp.bfloat16),
            pltpu.VMEM((groups,) + block, jnp.float32),
            pltpu.VMEM((groups,) + block, jnp.int16),
            pltpu.VMEM((groups, 8, width), jnp.float32),
            pltpu.VMEM((groups,) + block, jnp.int16),
            pltpu.VMEM((groups, 8, width), jnp.float32),
            pltpu.VMEM((groups,) + block, jnp.int16),
            pltpu.VMEM((groups, 8, width), jnp.float32),
            pltpu.VMEM((groups,) + block, jnp.int16),
            pltpu.VMEM((groups, 8, width), jnp.float32),
            pltpu.VMEM((groups, PAIR, rows, width), jnp.float32),
            pltpu.VMEM((groups, PAIR, rows, width), jnp.float32),
            dma((4,)),
            dma((groups,)),
            dma((groups,)), dma((groups,)),
            dma((groups,)), dma((groups,)),
            dma((members,)), dma((members,)),
            dma((groups, PAIR)), dma((groups, PAIR)),
            dma((groups,)), dma((groups,)),
            dma((groups,)), dma((groups,)),
            dma((groups,)), dma((groups,)),
            dma((groups,)), dma((groups,)),
        ],
        compiler_params=pltpu.CompilerParams(collective_id=0, has_side_effects=True, vmem_limit_bytes=VMEM_LIMIT),
        name="poisson_gradient",
    )(
        activity, histo_counts, background,
        jnp.swapaxes(blur_values, 2, 3).reshape(views * taps, band, width), jnp.swapaxes(band_start, 0, 1),
    )


def solution(mesh):
    placed = (
        P(("parts", "view"), "slab", None),
        P(("parts", "view"), None, "slab", None),
        P(("parts", "view"), "slab", None),
        P("view", None, None, None),
        P("view", None, None),
    )
    return jax.shard_map(
        per_device,
        mesh=mesh,
        in_specs=placed,
        out_specs=P(("parts", "view"), "slab", None),
        check_vma=False,
    )
```

```python
import functools

import jax
import jax.numpy as jnp
from jax import lax
from jax.experimental import pallas as pl
from jax.experimental.pallas import tpu as pltpu
from jax.sharding import PartitionSpec as P

MESH = pl.DeviceIdType.MESH
PAIR = 2
SLABS = 2


CODE_MAX = 32767.0
TINY = 1e-30
VMEM_LIMIT = 63 << 20


def encode(block):
    top = jnp.max(jnp.abs(block), axis=(0, 1), keepdims=False)[None, :]
    scale = jnp.where(top > TINY, CODE_MAX / jnp.maximum(top, TINY), 0.0)
    code = jnp.round(block * scale[None]).astype(jnp.int32).astype(jnp.int16)
    return code, jnp.broadcast_to(top * (1.0 / CODE_MAX), (8, block.shape[2]))


def decode(code, unit):
    return code.astype(jnp.int32).astype(jnp.float32) * unit[None, 0:1, :]


def kernel(
    groups, act_hbm, counts_ref, back_hbm, values_hbm, starts_hbm, out_ref,
    act_ref, back_ref, values_ref, starts_ref,
    acts, edges, edge_own, counts, forward_w, backward_w, kept, part_code, part_unit, pair_code, pair_unit, sum_code, sum_unit, owner_code, owner_unit, halo_out, halo_in,
    load_sem, counts_sem, line_send, line_recv, pair_send, pair_recv, edge_send, edge_recv,
    halo_send, halo_recv, part_send, part_recv, sum_send, sum_recv, part_unit_send, part_unit_recv, sum_unit_send, sum_unit_recv,
):
    part = lax.axis_index("parts")
    view = lax.axis_index("view")
    slab = lax.axis_index("slab")
    members = groups * PAIR
    last = groups - 1
    hi = view // PAIR
    lo = view % PAIR
    other = 1 - lo
    rows, slices, width = act_ref.shape
    views = back_ref.shape[0]
    taps = values_ref.shape[0] // views
    group_rows = PAIR * rows

    def at(hi_index, lo_index, slab_index):
        return (part, hi_index * PAIR + lo_index, slab_index)

    def met(step):
        key = (groups - step) % groups
        index, unit = 0, 1
        while unit < groups:
            index += ((hi // unit + key // unit) % 2) * unit
            unit *= 2
        return index

    barrier = pltpu.get_barrier_semaphore()
    for step in range(members):
        pl.semaphore_signal(
            barrier, inc=1, device_id=(part, lax.rem(view + step, members), 1 - slab), device_id_type=MESH
        )
    for step in range(1, groups):
        pl.semaphore_signal(barrier, inc=1, device_id=at(met(step), lo, slab), device_id_type=MESH)
    pl.semaphore_signal(barrier, inc=1, device_id=at(hi, other, slab), device_id_type=MESH)
    pl.semaphore_signal(barrier, inc=1, device_id=at(met(last), other, slab), device_id_type=MESH)

    def counts_copy(step):
        first = pl.multiple_of(met(step) * group_rows, group_rows)
        return pltpu.make_async_copy(
            counts_ref.at[:, pl.ds(first, group_rows)], counts.at[step], counts_sem.at[step]
        )

    loads = [
        pltpu.make_async_copy(source, target, load_sem.at[index])
        for index, (source, target) in enumerate(
            ((values_hbm, values_ref), (starts_hbm, starts_ref), (act_hbm, act_ref), (back_hbm, back_ref))
        )
    ]
    for load in loads:
        load.start()
    for step in range(groups):
        counts_copy(step).start()
    for load in loads:
        load.wait()
    own = act_ref[...]
    own_wide = own.astype(jnp.float32)
    edge_own[...] = jnp.where(slab == 0, own_wide[:, slices - 1, :], own_wide[:, 0, :]).astype(jnp.bfloat16)
    acts[view] = own

    def build(which):
        view_index, tap = which // taps, which % taps
        start = starts_ref[tap, view_index : view_index + 1, :]
        turned = jnp.concatenate(
            [values_ref[which].astype(jnp.float32), jnp.zeros((8, width), jnp.float32)], axis=0
        )
        shift = 1
        while shift < 8:
            turned = jnp.where((start & shift) != 0, pltpu.roll(turned, shift, axis=0), turned)
            shift *= 2
        while shift < width:
            extra = min(shift, width - turned.shape[0])
            plain = jnp.concatenate([turned, jnp.zeros((extra, width), jnp.float32)], axis=0)
            moved = jnp.concatenate([jnp.zeros((shift, width), jnp.float32), turned], axis=0)[: plain.shape[0]]
            turned = jnp.where((start & shift) != 0, moved, plain)
            shift *= 2
        forward_w[tap * width : (tap + 1) * width, view_index * width : (view_index + 1) * width] = (
            turned.astype(jnp.bfloat16)
        )
        backward_w[view_index * width : (view_index + 1) * width, tap * width : (tap + 1) * width] = (
            turned.T.astype(jnp.bfloat16)
        )

    total = views * taps
    for which in range(total):
        build(which)

    pl.semaphore_wait(barrier, members + groups + 1)

    def pair_copy(step, source):
        return pltpu.make_async_remote_copy(
            src_ref=source, dst_ref=acts.at[met(step) * PAIR + lo],
            send_sem=pair_send.at[step], recv_sem=pair_recv.at[step],
            device_id=at(hi, other, slab), device_id_type=MESH,
        )

    def near_copy():
        return pltpu.make_async_remote_copy(
            src_ref=acts.at[hi * PAIR + other], dst_ref=acts.at[hi * PAIR + other],
            send_sem=pair_send.at[last], recv_sem=pair_recv.at[last],
            device_id=at(met(last), lo, slab), device_id_type=MESH,
        )

    def line_copy(step):
        return pltpu.make_async_remote_copy(
            src_ref=act_ref, dst_ref=acts.at[view],
            send_sem=line_send.at[step], recv_sem=line_recv.at[step],
            device_id=at(met(step), lo, slab), device_id_type=MESH,
        )

    def edge_copy(step):
        return pltpu.make_async_remote_copy(
            src_ref=edge_own, dst_ref=edges.at[view],
            send_sem=edge_send.at[step], recv_sem=edge_recv.at[step],
            device_id=at(met(step // PAIR), (lo + step % PAIR) % PAIR, 1 - slab), device_id_type=MESH,
        )

    pair_copy(0, act_ref).start()
    for step in range(1, groups):
        line_copy(step).start()
    for step in range(members):
        edge_copy(step).start()

    slice_at = lax.broadcasted_iota(jnp.int32, (group_rows, slices, width), 1)
    inner = jnp.where(slab == 0, slices - 1, 0)

    def halo_copies(step):
        return [
            pltpu.make_async_remote_copy(
                src_ref=halo_out.at[step, keeper], dst_ref=halo_in.at[step, index],
                send_sem=halo_send.at[step, index], recv_sem=halo_recv.at[step, index],
                device_id=at(hi, keeper, 1 - slab), device_id_type=MESH,
            )
            for index, keeper in enumerate((lo, other))
        ]

    def part_copies(step, target):
        return [
            pltpu.make_async_remote_copy(
                src_ref=source.at[step], dst_ref=landing.at[step],
                send_sem=send.at[step], recv_sem=recv.at[step],
                device_id=at(target, other, slab), device_id_type=MESH,
            )
            for source, landing, send, recv in (
                (part_unit, pair_unit, part_unit_send, part_unit_recv),
                (part_code, pair_code, part_send, part_recv),
            )
        ]

    def sum_copies(step):
        return [
            pltpu.make_async_remote_copy(
                src_ref=source.at[step], dst_ref=target.at[step],
                send_sem=send.at[step], recv_sem=recv.at[step],
                device_id=at(met(step), lo, slab), device_id_type=MESH,
            )
            for source, target, send, recv in (
                (sum_unit, owner_unit, sum_unit_send, sum_unit_recv),
                (sum_code, owner_code, sum_send, sum_recv),
            )
        ]

    def relay(step):
        line_copy(step).wait_recv()
        pair_copy(step, acts.at[met(step) * PAIR + lo]).start()

    def kept_sum(step):
        for copy in halo_copies(step):
            copy.wait_recv()
        halo = (halo_in[step, 0] + halo_in[step, 1]).reshape(rows, 1, width)
        return kept[step] + jnp.where(slice_at[:rows] == inner, halo, 0.0)

    def pair_part(step):
        for copy in part_copies(step, hi):
            copy.wait_recv()
        return decode(pair_code[step], pair_unit[step])

    def pass_on(step, value):
        sum_code[step], sum_unit[step] = encode(value)
        for copy in sum_copies(step):
            copy.start()

    def one_group(step, carry):
        group = met(step)
        for which in range(PAIR):
            edge_copy(step * PAIR + which).wait_recv()
        pair_copy(step, act_ref).wait_recv()

        @pl.when(step == 0)
        def _():
            near_copy().start()

        @pl.when(step == last)
        def _():
            line_copy(last).wait_recv()

        image = acts[pl.ds(group * PAIR, PAIR)].astype(jnp.float32).reshape(group_rows, slices, width)
        edge = edges[pl.ds(group * PAIR, PAIR)].astype(jnp.float32).reshape(group_rows, 1, width)
        lower = jnp.where(slice_at == 0, jnp.where(slab == 0, 0.0, edge), pltpu.roll(image, 1, axis=1))
        upper = jnp.where(
            slice_at == slices - 1, jnp.where(slab == 0, edge, 0.0), pltpu.roll(image, slices - 1, axis=1)
        )
        stacked = jnp.concatenate(
            [x.reshape(-1, width).astype(jnp.bfloat16) for x in (lower, image, upper)], axis=1
        )
        summed = jnp.dot(stacked, forward_w[...], preferred_element_type=jnp.float32)
        counts_copy(step).wait()
        ratios = []
        ratio_edges = []
        for view_index in range(views):
            expected = (
                summed[:, view_index * width : (view_index + 1) * width].reshape(group_rows, slices, width)
                + back_ref[view_index].astype(jnp.float32)[None]
            )
            ratio = counts[step, view_index].astype(jnp.float32) / expected - 1.0
            ratio_edges.append(
                jnp.where(slab == 0, ratio[:, slices - 1, :], ratio[:, 0, :]).astype(jnp.bfloat16)
            )
            ratios.append(ratio.reshape(-1, width).astype(jnp.bfloat16))
        outer = pl.multiple_of((1 - slab) * ((taps - 1) * width), width)
        halo_out[step] = jnp.dot(
            jnp.concatenate(ratio_edges, axis=1), backward_w[:, pl.ds(outer, width)],
            preferred_element_type=jnp.float32,
        ).reshape(PAIR, rows, width)
        for copy in halo_copies(step):
            copy.start()
        spread = jnp.dot(
            jnp.concatenate(ratios, axis=1), backward_w[...], preferred_element_type=jnp.float32
        ).reshape(group_rows, slices, taps * width)
        from_upper = pltpu.roll(spread[:, :, :width], slices - 1, axis=1)
        from_lower = pltpu.roll(spread[:, :, 2 * width :], 1, axis=1)
        from_upper = jnp.where(slice_at == slices - 1, 0.0, from_upper)
        from_lower = jnp.where(slice_at == 0, 0.0, from_lower)
        spread_sum = (spread[:, :, width : 2 * width] + from_upper + from_lower).reshape(
            PAIR, rows, slices, width
        )
        kept[step] = jnp.where(lo == 0, spread_sum[0], spread_sum[1])
        part_code[step], part_unit[step] = encode(jnp.where(lo == 0, spread_sum[1], spread_sum[0]))

        @pl.when(step == 0)
        def _():
            for later in range(1, last):
                relay(later)

        @pl.when(step < last)
        def _():
            for copy in part_copies(step, hi):
                copy.start()

        @pl.when(step == last)
        def _():
            for copy in part_copies(step, met(last)):
                copy.start()

        @pl.when(step > 1)
        def _():
            pass_on(step - 1, kept_sum(step - 1) + pair_part(step - 1))

        return carry

    lax.fori_loop(0, groups, one_group, 0)
    pass_on(last, kept_sum(last))
    gradient = kept_sum(0) + pair_part(0)
    for step in range(1, groups):
        for copy in sum_copies(step):
            copy.wait_recv()
        gradient = gradient + decode(owner_code[step], owner_unit[step])
    out_ref[...] = gradient + pair_part(last)

    for step in range(1, groups):
        line_copy(step).wait_send()
        for copy in sum_copies(step):
            copy.wait_send()
    for step in range(groups):
        pair_copy(step, act_ref).wait_send()
        for copy in halo_copies(step):
            copy.wait_send()
        for copy in part_copies(step, hi):
            copy.wait_send()
    for step in range(members):
        edge_copy(step).wait_send()


def per_device(activity, histo_counts, background, blur_values, band_start):
    members = lax.axis_size("view")
    groups = members // PAIR
    rows, slices, width = activity.shape
    views, taps, _, band = blur_values.shape
    group_rows = PAIR * rows
    dma = pltpu.SemaphoreType.DMA
    block = (rows, slices, width)
    vmem = pl.BlockSpec(memory_space=pltpu.VMEM)
    return pl.pallas_call(
        functools.partial(kernel, groups),
        out_shape=jax.ShapeDtypeStruct(block, jnp.float32),
        in_specs=[pl.BlockSpec(memory_space=pl.ANY)] * 5,
        out_specs=vmem,
        scratch_shapes=[
            pltpu.VMEM(block, jnp.bfloat16),
            pltpu.VMEM(background.shape, jnp.bfloat16),
            pltpu.VMEM((views * taps, band, width), jnp.bfloat16),
            pltpu.VMEM((taps, views, width), jnp.int32),
            pltpu.VMEM((members,) + block, jnp.bfloat16),
            pltpu.VMEM((members, rows, width), jnp.bfloat16),
            pltpu.VMEM((rows, width), jnp.bfloat16),
            pltpu.VMEM((groups, views, group_rows, slices, width), jnp.int32),
            pltpu.VMEM((taps * width, views * width), jnp.bfloat16),
            pltpu.VMEM((views * width, taps * width), jnp.bfloat16),
            pltpu.VMEM((groups,) + block, jnp.float32),
            pltpu.VMEM((groups,) + block, jnp.int16),
            pltpu.VMEM((groups, 8, width), jnp.float32),
            pltpu.VMEM((groups,) + block, jnp.int16),
            pltpu.VMEM((groups, 8, width), jnp.float32),
            pltpu.VMEM((groups,) + block, jnp.int16),
            pltpu.VMEM((groups, 8, width), jnp.float32),
            pltpu.VMEM((groups,) + block, jnp.int16),
            pltpu.VMEM((groups, 8, width), jnp.float32),
            pltpu.VMEM((groups, PAIR, rows, width), jnp.float32),
            pltpu.VMEM((groups, PAIR, rows, width), jnp.float32),
            dma((4,)),
            dma((groups,)),
            dma((groups,)), dma((groups,)),
            dma((groups,)), dma((groups,)),
            dma((members,)), dma((members,)),
            dma((groups, PAIR)), dma((groups, PAIR)),
            dma((groups,)), dma((groups,)),
            dma((groups,)), dma((groups,)),
            dma((groups,)), dma((groups,)),
            dma((groups,)), dma((groups,)),
        ],
        compiler_params=pltpu.CompilerParams(collective_id=0, has_side_effects=True, vmem_limit_bytes=VMEM_LIMIT),
        name="poisson_gradient",
    )(
        activity, histo_counts, background,
        jnp.swapaxes(blur_values, 2, 3).reshape(views * taps, band, width), jnp.swapaxes(band_start, 0, 1),
    )


def solution(mesh):
    placed = (
        P(("parts", "view"), "slab", None),
        P(("parts", "view"), None, "slab", None),
        P(("parts", "view"), "slab", None),
        P("view", None, None, None),
        P("view", None, None),
    )
    return jax.shard_map(
        per_device,
        mesh=mesh,
        in_specs=placed,
        out_specs=P(("parts", "view"), "slab", None),
        check_vma=False,
    )
```
